32 devices in a mesh: pipe: 4 (over x, core), row: 4 (over z), col: 2 (over y).
Axes of the slice: x: 2, y: 2, z: 4, core: 2. Of those that a mesh axis runs over, the one named last changes fastest.
Arguments:
- handoff: bfloat16 [4, 256, 12288], P('pipe', 'col', 'row'), may hold values from -1200 to 1200
- norm_gain: float32 [4, 12288], P('pipe', 'row'), may hold values from 0.1 to 1.9
- norm_shift: float32 [4, 12288], P('pipe', 'row'), may hold values from -3 to 3
- up_weight: bfloat16 [4, 12288, 24576], P('pipe', 'row', 'col'), may hold values from -0.0546875 to 0.0546875
- up_bias: float32 [4, 24576], P('pipe', 'col'), may hold values from -3 to 3
Outputs:
- hidden: bfloat16 [4, 256, 24576], P('pipe', 'row', 'col')
The draws below stay inside these ranges and needn't reach their ends.
All inputs are finite; a program needn't handle non-finite values.
Results may differ from the reference program's by a relative error of at most 0.018.
Values may be sent and summed in bfloat16 or wider, within the bound.
A program may use at most 128 MiB of HBM per device.

```python
import math
import jax
import jax.numpy as jnp
from jax import lax

D = 12288
FF = 24576
MICRO = 256
SECTIONS = 4
FEATURE_BLOCKS = 4


def draw_handoff(key, part):
    key_rows, key_cols, key_jitter, key_offset = jax.random.split(key, 4)
    position = jnp.arange(D, dtype=jnp.float32) / D
    row_scale = jnp.exp(jax.random.uniform(key_rows, (SECTIONS, MICRO, 1), jnp.float32, 0.0, math.log(10.0)))
    feature_ramp = jnp.exp(math.log(3.0) * position)
    feature_spread = jnp.exp(jax.random.uniform(key_cols, (SECTIONS, 1, D), jnp.float32, 0.0, math.log(10.0)))
    jitter = jnp.clip(jax.random.normal(key_jitter, (SECTIONS, MICRO, D), jnp.float32), -3.0, 3.0)
    offset = jax.random.uniform(key_offset, (SECTIONS, MICRO, 1), jnp.float32, -1.0, 1.0)
    values = row_scale * feature_ramp * feature_spread * (jitter + offset)
    return values.astype(jnp.bfloat16)


def levels(own_key, shape, pieces, low, high):
    factor_of = 1.0
    for dim, parts in pieces:
        heights = jax.random.uniform(jax.random.fold_in(jax.random.fold_in(own_key, 6), dim), (parts,), jnp.float32, low / len(pieces), high / len(pieces))
        factor_of = factor_of * jnp.repeat(jnp.exp(heights), shape[dim] // parts).reshape((-1,) + (1,) * (len(shape) - 1 - dim))
    return factor_of


def normal_values(key, dims, deviation, bound, cuts=(), held_as=jnp.bfloat16):
    loudness = levels(key, dims, cuts, -0.22, 0.18) if cuts else 1.0
    drawn = jax.random.normal(key, dims, jnp.float32) * deviation * loudness
    return jnp.minimum(jnp.maximum(drawn, -bound), bound).astype(held_as)


def setup_inputs(seed: int = 0) -> dict:
    arg_keys = jax.random.split(jax.random.key(seed), 6)
    handoff = draw_handoff(jax.random.fold_in(arg_keys[5], 71), 0)
    norm_gain = jnp.clip(1.0 + 0.18 * jax.random.normal(arg_keys[1], (SECTIONS, D), jnp.float32), 0.1, 1.9)
    norm_shift = normal_values(arg_keys[2], (SECTIONS, D), 0.5, 3.0, ((0, 4), (1, 4)), jnp.float32)
    up_weight = normal_values(arg_keys[3], (SECTIONS, D, FF), D ** -0.5, 0.0546875, ((0, 4), (1, 4), (2, 2)))
    up_bias = normal_values(arg_keys[4], (SECTIONS, FF), 0.5, 3.0, ((0, 4), (1, 2)), jnp.float32)
    return dict(handoff=handoff, norm_gain=norm_gain, norm_shift=norm_shift, up_weight=up_weight, up_bias=up_bias)


epsilon = 1e-05

def one_section(inputs):
    arrived, norm_gain, norm_shift, up_weight, up_bias = inputs
    values = arrived.astype(jnp.float32)
    feature_count = values.shape[1]
    center = lax.optimization_barrier(jnp.sum(values, axis=1, keepdims=True)) / feature_count
    squares = lax.optimization_barrier(jnp.sum(values * values, axis=1, keepdims=True)) / feature_count
    inverse = lax.rsqrt(squares - center * center + epsilon)
    normed = ((values - center) * inverse * norm_gain + norm_shift).astype(jnp.bfloat16)
    block_width = feature_count // FEATURE_BLOCKS
    running = jnp.zeros((normed.shape[0], up_weight.shape[1]), jnp.float32)
    for block_index in range(FEATURE_BLOCKS):
        lower = block_index * block_width
        partial_value = jnp.dot(normed[:, lower:lower + block_width], up_weight[lower:lower + block_width], preferred_element_type=jnp.float32)
        rounded = lax.optimization_barrier(partial_value.astype(jnp.bfloat16))
        running = running + rounded.astype(jnp.float32)
    preact = running + up_bias
    return jax.nn.gelu(preact, approximate=True).astype(jnp.bfloat16)

def reference(handoff, norm_gain, norm_shift, up_weight, up_bias):
    arrived = jnp.roll(handoff, 1, axis=0)
    return lax.map(one_section, (arrived, norm_gain, norm_shift, up_weight, up_bias))
```

```python
import functools

import jax
import jax.numpy as jnp
from jax import lax
from jax.experimental import pallas as pl
from jax.experimental.pallas import tpu as pltpu
from jax.sharding import PartitionSpec as P

epsilon = 1e-05
MESH = pl.DeviceIdType.MESH
CHUNK = 1024
SUB = 512
SLOTS = 3
AHEAD = 4
EVERY = 3
FIRST = 3


def section_kernel(
    stages, rows, cols,
    own_ref, gain_ref, shift_ref, weight_ref, bias_ref, out_ref,
    landed, stats_out, stats_in, normed, weights, partial, received,
    weight_sem, own_send, own_recv, stat_send, stat_recv, part_send, part_recv,
):
    pipe, me, col = lax.axis_index("pipe"), lax.axis_index("row"), lax.axis_index("col")
    after = lax.rem(pipe + 1, stages)
    before = lax.rem(pipe + stages - 1, stages)
    tokens, depth = own_ref.shape
    chunks, micro, width = partial.shape
    per_group = rows // cols
    block = tokens // per_group
    feature_count = depth * rows
    last = rows - 1
    ahead = min(AHEAD, chunks // 2)
    lag = (ahead + 1) // 2
    steps = chunks + ahead
    turns = chunks + lag + max(rows - 3, 0)
    inner = (me > 0) & (me < last)

    def weight_copy(step):
        chunk, slot = lax.rem(step, chunks), lax.rem(step, SLOTS)
        columns = pl.ds(pl.multiple_of(chunk * width, width), width)
        return pltpu.make_async_copy(weight_ref.at[:, columns], weights.at[slot], weight_sem.at[slot])

    for step in range(min(SLOTS, steps)):
        weight_copy(step).start()

    barrier = pltpu.get_barrier_semaphore()

    def greet(i, carry):
        pl.semaphore_signal(
            barrier, inc=1, device_id=(before, i // cols, lax.rem(i, cols)), device_id_type=MESH
        )
        return carry

    lax.fori_loop(0, rows * cols, greet, 0)

    @pl.when(me > 0)
    def _():
        pl.semaphore_signal(barrier, inc=1, device_id=(pipe, me - 1, col), device_id_type=MESH)

    @pl.when(me < last)
    def _():
        pl.semaphore_signal(barrier, inc=1, device_id=(pipe, me + 1, col), device_id_type=MESH)

    values = own_ref[...].astype(jnp.float32)
    total = jnp.sum(values, axis=1, keepdims=True)
    squares = jnp.sum(values * values, axis=1, keepdims=True)
    lane = lax.broadcasted_iota(jnp.int32, (tokens, 128), 1)
    both = jnp.where(lane == 0, total, jnp.where(lane == 1, squares, 0.0))
    if tokens < 128:
        both = jnp.concatenate([both, jnp.zeros((128 - tokens, 128), jnp.float32)], axis=0)
    stats_out[...] = both.T[:8]

    neighbours = (me > 0).astype(jnp.int32) + (me < last).astype(jnp.int32)
    pl.semaphore_wait(barrier, rows * cols + neighbours)

    def own_copy(i):
        return pltpu.make_async_remote_copy(
            src_ref=own_ref, dst_ref=landed.at[col], send_sem=own_send.at[i], recv_sem=own_recv.at[col],
            device_id=(after, me, i), device_id_type=MESH,
        )

    def stat_copy(i):
        return pltpu.make_async_remote_copy(
            src_ref=stats_out, dst_ref=stats_in.at[col, me], send_sem=stat_send.at[i],
            recv_sem=stat_recv.at[col, me],
            device_id=(after, i // cols, lax.rem(i, cols)), device_id_type=MESH,
        )

    def start_stat(i, carry):
        stat_copy(i).start()
        return carry

    def start_own(i, carry):
        own_copy(lax.rem(col + i, cols)).start()
        return carry

    lax.fori_loop(0, rows * cols, start_stat, 0)
    lax.fori_loop(0, cols, start_own, 0)

    def to_normed(place, carry):
        group = lax.rem(col + place, cols)

        def wait_stat(z, carry):
            pltpu.make_async_remote_copy(
                src_ref=stats_out, dst_ref=stats_in.at[group, z], send_sem=stat_send.at[0],
                recv_sem=stat_recv.at[group, z], device_id=(after, me, col), device_id_type=MESH,
            ).wait_recv()
            return carry + stats_in[group, z]

        sums = lax.fori_loop(0, rows, wait_stat, jnp.zeros((8, 128), jnp.float32))
        by_token = jnp.concatenate([sums, jnp.zeros((120, 128), jnp.float32)], axis=0).T[:tokens]
        center = by_token[:, 0:1] / feature_count
        inverse = lax.rsqrt(by_token[:, 1:2] / feature_count - center * center + epsilon)
        pltpu.make_async_remote_copy(
            src_ref=own_ref, dst_ref=landed.at[group], send_sem=own_send.at[0],
            recv_sem=own_recv.at[group], device_id=(after, me, col), device_id_type=MESH,
        ).wait_recv()
        lines = pl.ds(pl.multiple_of(place * tokens, tokens), tokens)
        piece = 256
        for lower in range(0, depth, piece):
            part = landed[group, :, lower:lower + piece].astype(jnp.float32)
            scaled = (part - center) * inverse * gain_ref[:, lower:lower + piece]
            normed[lines, lower:lower + piece] = (scaled + shift_ref[:, lower:lower + piece]).astype(jnp.bfloat16)
        return carry

    def place_of(b):
        return lax.rem(b // per_group - col + cols, cols)

    def rows_of(b):
        return pl.ds(pl.multiple_of(place_of(b) * tokens + lax.rem(b, per_group) * block, block), block)

    def send(chunk, b, target, place):
        return pltpu.make_async_remote_copy(
            src_ref=partial.at[chunk, rows_of(b)], dst_ref=received.at[chunk, place],
            send_sem=part_send.at[chunk, b], recv_sem=part_recv.at[chunk, place],
            device_id=(pipe, target, col), device_id_type=MESH,
        )

    def chunk_of(b, index):
        return jnp.where(place_of(b) == 0, index, lax.rem(index + ahead, chunks))

    def relay(chunk, b):
        up = b > me
        place = jnp.where(up, b + 1, b)
        send(chunk, b, me, place).wait_recv()
        own = partial[chunk, rows_of(b)].astype(jnp.float32)
        partial[chunk, rows_of(b)] = (own + received[chunk, place].astype(jnp.float32)).astype(jnp.bfloat16)
        send(chunk, b, jnp.where(up, me + 1, me - 1), place).start()

    def turn_body(turn, carry):
        def one(i, carry):
            b = jnp.where(lax.rem(i, 2) == 0, last - i // 2, i // 2)
            hops = jnp.where(b > me, me - 1, last - 1 - me)
            index = turn - hops - jnp.where(place_of(b) == 0, 0, lag)

            @pl.when((b != me) & (index >= 0) & (index < chunks))
            def _():
                relay(chunk_of(b, index), b)

            return carry

        return lax.fori_loop(0, rows, one, carry)

    near = jnp.where(me == 0, 1, last - 1)
    beside = jnp.where(me == 0, 1, last - 1)

    def end_send(chunk, b):
        send(chunk, b, beside, jnp.where(me == 0, b + 1, b)).start()

    def end_sends(step, carry):
        chunk = lax.rem(step, chunks)

        def one(i, carry):
            b = jnp.where(me == 0, last - i, i)
            ready = jnp.where(place_of(b) == 0, step < chunks, step >= ahead)
            held = (b == near) & (step >= ahead) & (step < chunks)

            @pl.when(ready & jnp.logical_not(held))
            def _():
                end_send(chunk, b)

            return carry

        return lax.fori_loop(0, last, one, carry)

    def step_body(step, carry):
        chunk, slot = lax.rem(step, chunks), lax.rem(step, SLOTS)

        @pl.when(step == ahead)
        def _():
            lax.fori_loop(1, cols, to_normed, 0)

        weight_copy(step).wait()

        def multiply(first, count):
            lines = pl.ds(first, count)
            for lower in range(0, width, SUB):
                product = jnp.dot(
                    normed[lines, :], weights[slot, :, lower:lower + SUB], preferred_element_type=jnp.float32
                )
                partial[chunk, lines, lower:lower + SUB] = product.astype(jnp.bfloat16)

        whole = (step >= ahead) & (step < chunks)

        @pl.when(whole)
        def _():
            multiply(0, micro)

        if micro == 2 * tokens:
            @pl.when(jnp.logical_not(whole))
            def _():
                multiply(pl.multiple_of(jnp.where(step < ahead, 0, tokens), tokens), tokens)
        else:
            @pl.when(step < ahead)
            def _():
                multiply(0, tokens)

            @pl.when(step >= chunks)
            def _():
                multiply(tokens, micro - tokens)

        @pl.when(step + SLOTS < steps)
        def _():
            weight_copy(step + SLOTS).start()

        @pl.when(jnp.logical_not(inner))
        def _():
            end_sends(step, 0)

        late = step - FIRST

        @pl.when(inner & (late >= 0) & (lax.rem(late + EVERY, EVERY) == 0))
        def _():
            turn_body(late // EVERY, 0)

        return carry

    to_normed(0, 0)
    lax.fori_loop(0, steps, step_body, 0)

    @pl.when(jnp.logical_not(inner))
    def _():
        def held_send(chunk, carry):
            end_send(chunk, near)
            return carry

        lax.fori_loop(ahead, chunks, held_send, 0)

    @pl.when(inner)
    def _():
        done = len([late for late in range(0, steps - FIRST) if late % EVERY == 0])
        lax.fori_loop(done, turns, turn_body, 0)

    natural = (place_of(me) == 0) | (me == 1) | (me == last - 1)

    def final(index, carry):
        chunk = jnp.where(natural, index, lax.rem(index + ahead, chunks))

        @pl.when(me > 0)
        def _():
            send(chunk, me, me, me + 1).wait_recv()

        @pl.when(me < last)
        def _():
            send(chunk, me, me, me).wait_recv()

        columns = pl.ds(pl.multiple_of(chunk * width, width), width)
        preact = partial[chunk, rows_of(me)].astype(jnp.float32) + bias_ref[:, columns]
        left = jnp.where(me > 0, received[chunk, me + 1].astype(jnp.float32), 0.0)
        right = jnp.where(me < last, received[chunk, me].astype(jnp.float32), 0.0)
        preact = preact + left + right
        out_ref[:, columns] = jax.nn.gelu(preact, approximate=True).astype(jnp.bfloat16)
        return carry

    lax.fori_loop(0, chunks, final, 0)

    def finish(i, carry):
        chunk, b = i // rows, lax.rem(i, rows)

        @pl.when(b != me)
        def _():
            send(chunk, b, me, b).wait_send()

        return carry

    lax.fori_loop(0, chunks * rows, finish, 0)

    def finish_stat(i, carry):
        stat_copy(i).wait_send()
        return carry

    def finish_own(i, carry):
        own_copy(i).wait_send()
        return carry

    lax.fori_loop(0, rows * cols, finish_stat, 0)
    lax.fori_loop(0, cols, finish_own, 0)


def local(stages, rows, cols, handoff, norm_gain, norm_shift, up_weight, up_bias):
    own = handoff[0]
    tokens, depth = own.shape
    hidden = up_weight.shape[2]
    width = min(CHUNK, hidden)
    chunks = hidden // width
    micro = tokens * cols
    block = micro // rows
    vmem = pl.BlockSpec(memory_space=pltpu.VMEM)
    result = pl.pallas_call(
        functools.partial(section_kernel, stages, rows, cols),
        out_shape=jax.ShapeDtypeStruct((block, hidden), jnp.bfloat16),
        in_specs=[vmem, vmem, vmem, pl.BlockSpec(memory_space=pl.ANY), vmem],
        out_specs=vmem,
        scratch_shapes=[
            pltpu.VMEM((cols, tokens, depth), jnp.bfloat16),
            pltpu.VMEM((8, 128), jnp.float32),
            pltpu.VMEM((cols, rows, 8, 128), jnp.float32),
            pltpu.VMEM((micro, depth), jnp.bfloat16),
            pltpu.VMEM((SLOTS, depth, width), jnp.bfloat16),
            pltpu.VMEM((chunks, micro, width), jnp.bfloat16),
            pltpu.VMEM((chunks, rows + 1, block, width), jnp.bfloat16),
            pltpu.SemaphoreType.DMA((SLOTS,)),
            pltpu.SemaphoreType.DMA((cols,)),
            pltpu.SemaphoreType.DMA((cols,)),
            pltpu.SemaphoreType.DMA((rows * cols,)),
            pltpu.SemaphoreType.DMA((cols, rows)),
            pltpu.SemaphoreType.DMA((chunks, rows)),
            pltpu.SemaphoreType.DMA((chunks, rows + 1)),
        ],
        compiler_params=pltpu.CompilerParams(
            collective_id=0, has_side_effects=True, vmem_limit_bytes=60 * 1024 * 1024
        ),
    )(own, norm_gain, norm_shift, up_weight[0], up_bias)
    return result[None]


def solution(mesh):
    in_specs = (
        P("pipe", "col", "row"),
        P("pipe", "row"),
        P("pipe", "row"),
        P("pipe", "row", "col"),
        P("pipe", "col"),
    )
    out_specs = P("pipe", "row", "col")
    sizes = mesh.shape["pipe"], mesh.shape["row"], mesh.shape["col"]
    return jax.shard_map(
        functools.partial(local, *sizes), mesh=mesh, in_specs=in_specs, out_specs=out_specs, check_vma=False
    )
```

```python
import functools

import jax
import jax.numpy as jnp
from jax import lax
from jax.experimental import pallas as pl
from jax.experimental.pallas import tpu as pltpu
from jax.sharding import PartitionSpec as P

epsilon = 1e-05
MESH = pl.DeviceIdType.MESH
CHUNK = 1024
SUB = 512
SLOTS = 5
AHEAD = 6
EVERY = 3
FIRST = 3


def section_kernel(
    stages, rows, cols,
    own_hbm, gain_hbm, shift_hbm, weight_ref, bias_hbm, out_ref,
    own_ref, gain_ref, shift_ref, bias_ref, landed, stats_out, stats_in, normed, weights, partial, received,
    input_sem, weight_sem, own_send, own_recv, pass_send, stat_send, stat_recv, part_send, part_recv,
):
    pipe, me, col = lax.axis_index("pipe"), lax.axis_index("row"), lax.axis_index("col")
    after = lax.rem(pipe + 1, stages)
    before = lax.rem(pipe + stages - 1, stages)
    tokens, depth = own_ref.shape
    chunks, micro, width = partial.shape
    per_group = rows // cols
    block = tokens // per_group
    feature_count = depth * rows
    last = rows - 1
    ahead = min(AHEAD, chunks // 2)
    lag = (ahead + 1) // 2
    steps = chunks + ahead
    turns = chunks + lag + max(rows - 3, 0)
    inner = (me > 0) & (me < last)
    crossed = lax.rem(pipe, 2) == 0
    direct = jnp.where(crossed, cols, 1)

    def weight_copy(step):
        chunk, slot = lax.rem(step, chunks), lax.rem(step, SLOTS)
        columns = pl.ds(pl.multiple_of(chunk * width, width), width)
        return pltpu.make_async_copy(weight_ref.at[:, columns], weights.at[slot], weight_sem.at[slot])

    def input_copy(i):
        source, target = ((own_hbm, own_ref), (gain_hbm, gain_ref), (shift_hbm, shift_ref), (bias_hbm, bias_ref))[i]
        return pltpu.make_async_copy(source, target, input_sem.at[i])

    for i in range(4):
        input_copy(i).start()

    barrier = pltpu.get_barrier_semaphore()

    def greet(i, carry):
        pl.semaphore_signal(
            barrier, inc=1, device_id=(before, i // cols, lax.rem(i, cols)), device_id_type=MESH
        )
        return carry

    lax.fori_loop(0, rows * cols, greet, 0)

    def greet_beside(i, carry):
        pl.semaphore_signal(barrier, inc=1, device_id=(pipe, me, lax.rem(col + i, cols)), device_id_type=MESH)
        return carry

    @pl.when(crossed)
    def _():
        lax.fori_loop(1, cols, greet_beside, 0)

    @pl.when(me > 0)
    def _():
        pl.semaphore_signal(barrier, inc=1, device_id=(pipe, me - 1, col), device_id_type=MESH)

    @pl.when(me < last)
    def _():
        pl.semaphore_signal(barrier, inc=1, device_id=(pipe, me + 1, col), device_id_type=MESH)

    for step in range(min(SLOTS, steps)):
        weight_copy(step).start()

    input_copy(0).wait()
    values = own_ref[...].astype(jnp.float32)
    total = jnp.sum(values, axis=1, keepdims=True)
    squares = jnp.sum(values * values, axis=1, keepdims=True)
    lane = lax.broadcasted_iota(jnp.int32, (tokens, 128), 1)
    both = jnp.where(lane == 0, total, jnp.where(lane == 1, squares, 0.0))
    if tokens < 128:
        both = jnp.concatenate([both, jnp.zeros((128 - tokens, 128), jnp.float32)], axis=0)
    stats_out[...] = both.T[:8]

    neighbours = (me > 0).astype(jnp.int32) + (me < last).astype(jnp.int32)
    pl.semaphore_wait(barrier, rows * cols + neighbours + jnp.where(crossed, cols - 1, 0))

    def own_copy(i):
        return pltpu.make_async_remote_copy(
            src_ref=own_ref, dst_ref=landed.at[col], send_sem=own_send.at[i], recv_sem=own_recv.at[col],
            device_id=(after, me, i), device_id_type=MESH,
        )

    def stat_copy(i):
        return pltpu.make_async_remote_copy(
            src_ref=stats_out, dst_ref=stats_in.at[col, me], send_sem=stat_send.at[i],
            recv_sem=stat_recv.at[col, me],
            device_id=(after, i // cols, lax.rem(i, cols)), device_id_type=MESH,
        )

    def start_stat(i, carry):
        stat_copy(i).start()
        return carry

    def start_own(i, carry):
        own_copy(lax.rem(col + i, cols)).start()
        return carry

    lax.fori_loop(0, rows * cols, start_stat, 0)
    lax.fori_loop(0, direct, start_own, 0)

    def pass_copy(i):
        return pltpu.make_async_remote_copy(
            src_ref=landed.at[col], dst_ref=landed.at[col], send_sem=pass_send.at[i], recv_sem=own_recv.at[col],
            device_id=(pipe, me, i), device_id_type=MESH,
        )

    def to_normed(place, carry):
        group = lax.rem(col + place, cols)

        def wait_stat(z, carry):
            pltpu.make_async_remote_copy(
                src_ref=stats_out, dst_ref=stats_in.at[group, z], send_sem=stat_send.at[0],
                recv_sem=stat_recv.at[group, z], device_id=(after, me, col), device_id_type=MESH,
            ).wait_recv()
            return carry + stats_in[group, z]

        sums = lax.fori_loop(0, rows, wait_stat, jnp.zeros((8, 128), jnp.float32))
        by_token = jnp.concatenate([sums, jnp.zeros((120, 128), jnp.float32)], axis=0).T[:tokens]
        center = by_token[:, 0:1] / feature_count
        inverse = lax.rsqrt(by_token[:, 1:2] / feature_count - center * center + epsilon)
        pltpu.make_async_remote_copy(
            src_ref=own_ref, dst_ref=landed.at[group], send_sem=own_send.at[0],
            recv_sem=own_recv.at[group], device_id=(after, me, col), device_id_type=MESH,
        ).wait_recv()

        @pl.when(crossed & (place == 0))
        def _():
            def start_pass(i, carry):
                pass_copy(lax.rem(col + i, cols)).start()
                return carry

            lax.fori_loop(1, cols, start_pass, 0)

        lines = pl.ds(pl.multiple_of(place * tokens, tokens), tokens)
        piece = 256
        for lower in range(0, depth, piece):
            part = landed[group, :, lower:lower + piece].astype(jnp.float32)
            scaled = (part - center) * inverse * gain_ref[:, lower:lower + piece]
            normed[lines, lower:lower + piece] = (scaled + shift_ref[:, lower:lower + piece]).astype(jnp.bfloat16)
        return carry

    def place_of(b):
        return lax.rem(b // per_group - col + cols, cols)

    def rows_of(b):
        return pl.ds(pl.multiple_of(place_of(b) * tokens + lax.rem(b, per_group) * block, block), block)

    def send(chunk, b, target, place):
        return pltpu.make_async_remote_copy(
            src_ref=partial.at[chunk, rows_of(b)], dst_ref=received.at[chunk, place],
            send_sem=part_send.at[chunk, b], recv_sem=part_recv.at[chunk, place],
            device_id=(pipe, target, col), device_id_type=MESH,
        )

    def chunk_of(b, index):
        return jnp.where(place_of(b) == 0, index, lax.rem(index + ahead, chunks))

    def relay(chunk, b):
        up = b > me
        place = jnp.where(up, b + 1, b)
        send(chunk, b, me, place).wait_recv()
        own = partial[chunk, rows_of(b)].astype(jnp.float32)
        partial[chunk, rows_of(b)] = (own + received[chunk, place].astype(jnp.float32)).astype(jnp.bfloat16)
        send(chunk, b, jnp.where(up, me + 1, me - 1), place).start()

    def turn_body(turn, carry):
        def one(i, carry):
            b = jnp.where(lax.rem(i, 2) == 0, last - i // 2, i // 2)
            hops = jnp.where(b > me, me - 1, last - 1 - me)
            index = turn - hops - jnp.where(place_of(b) == 0, 0, lag)

            @pl.when((b != me) & (index >= 0) & (index < chunks))
            def _():
                relay(chunk_of(b, index), b)

            return carry

        return lax.fori_loop(0, rows, one, carry)

    near = jnp.where(me == 0, 1, last - 1)
    beside = jnp.where(me == 0, 1, last - 1)

    def end_send(chunk, b):
        send(chunk, b, beside, jnp.where(me == 0, b + 1, b)).start()

    def end_sends(step, carry):
        chunk = lax.rem(step, chunks)

        def one(i, carry):
            b = jnp.where(me == 0, last - i, i)
            ready = jnp.where(place_of(b) == 0, step < chunks, step >= ahead)
            held = (b == near) & (step >= ahead) & (step < chunks)

            @pl.when(ready & jnp.logical_not(held))
            def _():
                end_send(chunk, b)

            return carry

        return lax.fori_loop(0, last, one, carry)

    def step_body(step, carry):
        chunk, slot = lax.rem(step, chunks), lax.rem(step, SLOTS)

        @pl.when(step == ahead)
        def _():
            lax.fori_loop(1, cols, to_normed, 0)

        weight_copy(step).wait()

        def multiply(first, count):
            lines = pl.ds(first, count)
            for lower in range(0, width, SUB):
                product = jnp.dot(
                    normed[lines, :], weights[slot, :, lower:lower + SUB], preferred_element_type=jnp.float32
                )
                partial[chunk, lines, lower:lower + SUB] = product.astype(jnp.bfloat16)

        whole = (step >= ahead) & (step < chunks)

        @pl.when(whole)
        def _():
            multiply(0, micro)

        if micro == 2 * tokens:
            @pl.when(jnp.logical_not(whole))
            def _():
                multiply(pl.multiple_of(jnp.where(step < ahead, 0, tokens), tokens), tokens)
        else:
            @pl.when(step < ahead)
            def _():
                multiply(0, tokens)

            @pl.when(step >= chunks)
            def _():
                multiply(tokens, micro - tokens)

        @pl.when(step + SLOTS < steps)
        def _():
            weight_copy(step + SLOTS).start()

        @pl.when(jnp.logical_not(inner))
        def _():
            end_sends(step, 0)

        late = step - FIRST

        @pl.when(inner & (late >= 0) & (lax.rem(late + EVERY, EVERY) == 0))
        def _():
            turn_body(late // EVERY, 0)

        return carry

    for i in range(1, 4):
        input_copy(i).wait()

    to_normed(0, 0)
    lax.fori_loop(0, steps, step_body, 0)

    @pl.when(jnp.logical_not(inner))
    def _():
        def held_send(chunk, carry):
            end_send(chunk, near)
            return carry

        lax.fori_loop(ahead, chunks, held_send, 0)

    @pl.when(inner)
    def _():
        done = len([late for late in range(0, steps - FIRST) if late % EVERY == 0])
        lax.fori_loop(done, turns, turn_body, 0)

    natural = (place_of(me) == 0) | (me == 1) | (me == last - 1)

    def final(index, carry):
        chunk = jnp.where(natural, index, lax.rem(index + ahead, chunks))

        @pl.when(me > 0)
        def _():
            send(chunk, me, me, me + 1).wait_recv()

        @pl.when(me < last)
        def _():
            send(chunk, me, me, me).wait_recv()

        columns = pl.ds(pl.multiple_of(chunk * width, width), width)
        preact = partial[chunk, rows_of(me)].astype(jnp.float32) + bias_ref[:, columns]
        left = jnp.where(me > 0, received[chunk, me + 1].astype(jnp.float32), 0.0)
        right = jnp.where(me < last, received[chunk, me].astype(jnp.float32), 0.0)
        preact = preact + left + right
        out_ref[:, columns] = jax.nn.gelu(preact, approximate=True).astype(jnp.bfloat16)
        return carry

    lax.fori_loop(0, chunks - 1, final, 0)

    def finish(i, carry):
        chunk, b = i // rows, lax.rem(i, rows)

        @pl.when(b != me)
        def _():
            send(chunk, b, me, b).wait_send()

        return carry


    def finish_stat(i, carry):
        stat_copy(i).wait_send()
        return carry

    def finish_own(i, carry):
        own_copy(lax.rem(col + i, cols)).wait_send()
        return carry

    def finish_pass(i, carry):
        pass_copy(lax.rem(col + i, cols)).wait_send()
        return carry

    lax.fori_loop(0, rows * cols, finish_stat, 0)
    lax.fori_loop(0, direct, finish_own, 0)

    @pl.when(crossed)
    def _():
        lax.fori_loop(1, cols, finish_pass, 0)

    @pl.when(inner)
    def _():
        lax.fori_loop(0, chunks * rows, finish, 0)

    final(chunks - 1, 0)

    @pl.when(jnp.logical_not(inner))
    def _():
        lax.fori_loop(0, chunks * rows, finish, 0)


def local(stages, rows, cols, handoff, norm_gain, norm_shift, up_weight, up_bias):
    own = handoff[0]
    tokens, depth = own.shape
    hidden = up_weight.shape[2]
    width = min(CHUNK, hidden)
    chunks = hidden // width
    micro = tokens * cols
    block = micro // rows
    result = pl.pallas_call(
        functools.partial(section_kernel, stages, rows, cols),
        out_shape=pltpu.VMEM((block, hidden), jnp.bfloat16),
        in_specs=[pl.BlockSpec(memory_space=pl.ANY)] * 5,
        out_specs=pl.BlockSpec(memory_space=pltpu.VMEM),
        scratch_shapes=[
            pltpu.VMEM((tokens, depth), jnp.bfloat16),
            pltpu.VMEM((1, depth), jnp.float32),
            pltpu.VMEM((1, depth), jnp.float32),
            pltpu.VMEM((1, hidden), jnp.float32),
            pltpu.VMEM((cols, tokens, depth), jnp.bfloat16),
            pltpu.VMEM((8, 128), jnp.float32),
            pltpu.VMEM((cols, rows, 8, 128), jnp.float32),
            pltpu.VMEM((micro, depth), jnp.bfloat16),
            pltpu.VMEM((SLOTS, depth, width), jnp.bfloat16),
            pltpu.VMEM((chunks, micro, width), jnp.bfloat16),
            pltpu.VMEM((chunks, rows + 1, block, width), jnp.bfloat16),
            pltpu.SemaphoreType.DMA((4,)),
            pltpu.SemaphoreType.DMA((SLOTS,)),
            pltpu.SemaphoreType.DMA((cols,)),
            pltpu.SemaphoreType.DMA((cols,)),
            pltpu.SemaphoreType.DMA((cols,)),
            pltpu.SemaphoreType.DMA((rows * cols,)),
            pltpu.SemaphoreType.DMA((cols, rows)),
            pltpu.SemaphoreType.DMA((chunks, rows)),
            pltpu.SemaphoreType.DMA((chunks, rows + 1)),
        ],
        compiler_params=pltpu.CompilerParams(
            collective_id=0, has_side_effects=True, vmem_limit_bytes=60 * 1024 * 1024
        ),
    )(own, norm_gain, norm_shift, up_weight[0], up_bias)
    return result[None]


def solution(mesh):
    in_specs = (
        P("pipe", "col", "row"),
        P("pipe", "row"),
        P("pipe", "row"),
        P("pipe", "row", "col"),
        P("pipe", "col"),
    )
    out_specs = P("pipe", "row", "col")
    sizes = mesh.shape["pipe"], mesh.shape["row"], mesh.shape["col"]
    return jax.shard_map(
        functools.partial(local, *sizes), mesh=mesh, in_specs=in_specs, out_specs=out_specs, check_vma=False
    )
```

```python
import functools

import jax
import jax.numpy as jnp
from jax import lax
from jax.experimental import pallas as pl
from jax.experimental.pallas import tpu as pltpu
from jax.sharding import PartitionSpec as P

epsilon = 1e-05
MESH = pl.DeviceIdType.MESH
CHUNK = 1024
SUB = 512
OPENING = 512
CLOSING = 3
SLOTS = 5
AHEAD = 6
AHEAD_CROSSED = 4
EVERY = 3
FIRST = 3


def section_kernel(
    stages, rows, cols,
    own_hbm, gain_hbm, shift_hbm, weight_ref, bias_hbm, out_ref,
    own_ref, gain_ref, shift_ref, bias_ref, landed, stats_out, stats_in, normed, weights, partial, received,
    input_sem, weight_sem, own_send, own_recv, pass_send, stat_send, stat_recv, part_send, part_recv,
):
    pipe, me, col = lax.axis_index("pipe"), lax.axis_index("row"), lax.axis_index("col")
    after = lax.rem(pipe + 1, stages)
    before = lax.rem(pipe + stages - 1, stages)
    tokens, depth = own_ref.shape
    chunks, micro, width = partial.shape
    per_group = rows // cols
    block = tokens // per_group
    feature_count = depth * rows
    last = rows - 1
    crossed = lax.rem(pipe, 2) == 0
    ahead = jnp.where(crossed, min(AHEAD_CROSSED, chunks // 2), min(AHEAD, chunks // 2))
    lag = (ahead + 1) // 2
    steps = chunks + ahead
    turns = chunks + lag + max(rows - 3, 0)
    inner = (me > 0) & (me < last)
    mine = me // per_group
    paired = per_group == 2
    sibling = 2 * mine + 1 - lax.rem(me, 2)
    assert per_group <= 2
    direct = jnp.where(crossed, cols, 1)

    def weight_copy(step):
        chunk, slot = lax.rem(step, chunks), lax.rem(step, min(SLOTS, chunks))
        columns = pl.ds(pl.multiple_of(chunk * width, width), width)
        return pltpu.make_async_copy(weight_ref.at[:, columns], weights.at[slot], weight_sem.at[slot])

    def input_copy(i):
        source, target = ((own_hbm, own_ref), (gain_hbm, gain_ref), (shift_hbm, shift_ref), (bias_hbm, bias_ref))[i]
        return pltpu.make_async_copy(source, target, input_sem.at[i])

    for i in range(4):
        input_copy(i).start()

    barrier = pltpu.get_barrier_semaphore()

    def greet(i, carry):
        pl.semaphore_signal(
            barrier, inc=1, device_id=(before, i // cols, lax.rem(i, cols)), device_id_type=MESH
        )
        return carry

    lax.fori_loop(0, rows * cols, greet, 0)

    def greet_beside(i, carry):
        pl.semaphore_signal(barrier, inc=1, device_id=(pipe, me, lax.rem(col + i, cols)), device_id_type=MESH)
        return carry

    @pl.when(crossed)
    def _():
        lax.fori_loop(1, cols, greet_beside, 0)

    @pl.when(me > 0)
    def _():
        pl.semaphore_signal(barrier, inc=1, device_id=(pipe, me - 1, col), device_id_type=MESH)

    @pl.when(me < last)
    def _():
        pl.semaphore_signal(barrier, inc=1, device_id=(pipe, me + 1, col), device_id_type=MESH)

    for step in range(min(SLOTS, chunks)):
        weight_copy(step).start()

    input_copy(0).wait()
    total = jnp.zeros((tokens, 128), jnp.float32)
    squares = jnp.zeros((tokens, 128), jnp.float32)
    for lower in range(0, depth, 128):
        values = own_ref[:, lower:lower + 128].astype(jnp.float32)
        total = total + values
        squares = squares + values * values
    total = jnp.sum(total, axis=1, keepdims=True)
    squares = jnp.sum(squares, axis=1, keepdims=True)
    lane = lax.broadcasted_iota(jnp.int32, (tokens, 128), 1)
    both = jnp.where(lane == 0, total, jnp.where(lane == 1, squares, 0.0))
    if tokens < 128:
        both = jnp.concatenate([both, jnp.zeros((128 - tokens, 128), jnp.float32)], axis=0)
    stats_out[...] = both.T[:8]

    neighbours = (me > 0).astype(jnp.int32) + (me < last).astype(jnp.int32)
    pl.semaphore_wait(barrier, rows * cols + neighbours + jnp.where(crossed, cols - 1, 0))

    def own_copy(i):
        return pltpu.make_async_remote_copy(
            src_ref=own_ref, dst_ref=landed.at[col], send_sem=own_send.at[i], recv_sem=own_recv.at[col],
            device_id=(after, me, i), device_id_type=MESH,
        )

    def stat_copy(i):
        return pltpu.make_async_remote_copy(
            src_ref=stats_out, dst_ref=stats_in.at[col, me], send_sem=stat_send.at[i],
            recv_sem=stat_recv.at[col, me],
            device_id=(after, i // cols, lax.rem(i, cols)), device_id_type=MESH,
        )

    def start_stat(i, carry):
        stat_copy(i).start()
        return carry

    def start_own(i, carry):
        own_copy(lax.rem(col + i, cols)).start()
        return carry

    lax.fori_loop(0, rows * cols, start_stat, 0)
    lax.fori_loop(0, direct, start_own, 0)

    def pass_copy(i):
        return pltpu.make_async_remote_copy(
            src_ref=landed.at[col], dst_ref=landed.at[col], send_sem=pass_send.at[i], recv_sem=own_recv.at[col],
            device_id=(pipe, me, i), device_id_type=MESH,
        )

    def to_normed(place, carry):
        group = lax.rem(col + place, cols)

        def wait_stat(z, carry):
            pltpu.make_async_remote_copy(
                src_ref=stats_out, dst_ref=stats_in.at[group, z], send_sem=stat_send.at[0],
                recv_sem=stat_recv.at[group, z], device_id=(after, me, col), device_id_type=MESH,
            ).wait_recv()
            return carry + stats_in[group, z]

        sums = lax.fori_loop(0, rows, wait_stat, jnp.zeros((8, 128), jnp.float32))
        by_token = jnp.concatenate([sums, jnp.zeros((120, 128), jnp.float32)], axis=0).T[:tokens]
        center = by_token[:, 0:1] / feature_count
        inverse = lax.rsqrt(by_token[:, 1:2] / feature_count - center * center + epsilon)
        pltpu.make_async_remote_copy(
            src_ref=own_ref, dst_ref=landed.at[group], send_sem=own_send.at[0],
            recv_sem=own_recv.at[group], device_id=(after, me, col), device_id_type=MESH,
        ).wait_recv()

        @pl.when(crossed & (place == 0))
        def _():
            def start_pass(i, carry):
                pass_copy(lax.rem(col + i, cols)).start()
                return carry

            lax.fori_loop(1, cols, start_pass, 0)

        lines = pl.ds(pl.multiple_of(place * tokens, tokens), tokens)
        piece = 256
        for lower in range(0, depth, piece):
            part = landed[group, :, lower:lower + piece].astype(jnp.float32)
            scaled = (part - center) * inverse * gain_ref[:, lower:lower + piece]
            normed[lines, lower:lower + piece] = (scaled + shift_ref[:, lower:lower + piece]).astype(jnp.bfloat16)
        return carry

    def place_of(group):
        return lax.rem(group - col + cols, cols)

    def lines_of(first, count):
        start = place_of(first // per_group) * tokens + lax.rem(first, per_group) * block
        return pl.ds(pl.multiple_of(start, block), count)

    def landing(first, count):
        return pl.ds(pl.multiple_of(first * block, block), count)

    def piece_copy(chunk, first, count, up, target, columns):
        place = first + jnp.where(up, 1, 0)
        return pltpu.make_async_remote_copy(
            src_ref=partial.at[chunk, lines_of(first, count), columns],
            dst_ref=received.at[chunk, landing(place, count), columns],
            send_sem=part_send.at[chunk, first], recv_sem=part_recv.at[chunk, place],
            device_id=(pipe, target, col), device_id_type=MESH,
        )

    everything = pl.ds(0, width)

    def unit(chunk, group, up, target, columns=everything):
        return piece_copy(chunk, group * per_group, tokens, up, target, columns)

    def single(chunk, b, up, target, columns=everything):
        return piece_copy(chunk, b, block, up, target, columns)

    def chunk_of(group, index):
        return jnp.where(place_of(group) == 0, index, lax.rem(index + ahead, chunks))

    def add_arrived(chunk, first, count, up):
        lines = lines_of(first, count)
        arrived = received[chunk, landing(first + jnp.where(up, 1, 0), count)]
        own = partial[chunk, lines].astype(jnp.float32)
        partial[chunk, lines] = (own + arrived.astype(jnp.float32)).astype(jnp.bfloat16)

    leads, trails = lax.rem(me, per_group) == 0, lax.rem(me, per_group) == per_group - 1

    def relay_unit(chunk, group):
        up = group > mine
        unit(chunk, group, up, me).wait_recv()
        add_arrived(chunk, group * per_group, tokens, up)
        unit(chunk, group, up, jnp.where(up, me + 1, me - 1)).start()

    def relay_sibling(chunk):
        up = sibling > me
        unit(chunk, mine, up, me).wait_recv()
        add_arrived(chunk, sibling, block, up)
        single(chunk, sibling, up, sibling).start()

    def turn_body(turn, carry):
        def one(i, carry):
            group = jnp.where(lax.rem(i, 2) == 0, cols - 1 - i // 2, i // 2)
            up = jnp.where(group == mine, sibling > me, group > mine)
            hops = jnp.where(up, me - 1, last - 1 - me)
            index = turn - hops - jnp.where(place_of(group) == 0, 0, lag)
            valid = (index >= 0) & (index < chunks)

            @pl.when(valid & (group != mine))
            def _():
                relay_unit(chunk_of(group, index), group)

            if paired:
                @pl.when(valid & (group == mine))
                def _():
                    relay_sibling(chunk_of(group, index))

            return carry

        return lax.fori_loop(0, cols, one, carry)

    upward = me == 0
    beside = jnp.where(upward, 1, last - 1)

    def end_unit(chunk, group, columns=everything):
        unit(chunk, group, upward, beside, columns).start()

    def end_single(chunk, columns=everything):
        single(chunk, sibling, upward, beside, columns).start()

    def end_sends(step, lead):
        chunk = lax.rem(step, chunks)

        def one(i, carry):
            group = jnp.where(upward, cols - 1 - i, i)
            ready = (place_of(group) == 0) == lead

            @pl.when(ready & (group != mine))
            def _():
                end_unit(chunk, group)

            if paired:
                @pl.when(ready & (group == mine) & ((step < ahead) | (step >= chunks)))
                def _():
                    end_single(chunk)

            return carry

        lax.fori_loop(0, cols, one, 0)

    def multiply(chunk, slot, first, count, lower, span):
        lines = pl.ds(first, count)
        product = jnp.dot(
            normed[lines, :], weights[slot, :, lower:lower + span], preferred_element_type=jnp.float32
        )
        partial[chunk, lines, lower:lower + span] = product.astype(jnp.bfloat16)

    def refill(step):
        @pl.when(step + min(SLOTS, chunks) < steps)
        def _():
            weight_copy(step + min(SLOTS, chunks)).start()

    def opening():
        weight_copy(0).wait()
        span = min(OPENING, width)
        for lower in range(0, width, span):
            multiply(0, 0, 0, tokens, lower, span)
            columns = pl.ds(lower, span)

            @pl.when(jnp.logical_not(inner) & (mine != col))
            def _():
                end_unit(0, col, columns)

            if paired:
                @pl.when(jnp.logical_not(inner) & (mine == col))
                def _():
                    end_single(0, columns)

        refill(0)

    def step_body(step, carry):
        chunk, slot = lax.rem(step, chunks), lax.rem(step, min(SLOTS, chunks))

        @pl.when(step == ahead)
        def _():
            lax.fori_loop(1, cols, to_normed, 0)

        weight_copy(step).wait()

        def part(which, carry):
            lead = which == 1
            if micro == 2 * tokens:
                first = pl.multiple_of(jnp.where(lead, 0, tokens), tokens)
                for lower in range(0, width, SUB):
                    multiply(chunk, slot, first, tokens, lower, SUB)
            else:
                @pl.when(lead)
                def _():
                    for lower in range(0, width, SUB):
                        multiply(chunk, slot, 0, tokens, lower, SUB)

                @pl.when(jnp.logical_not(lead))
                def _():
                    for lower in range(0, width, SUB):
                        multiply(chunk, slot, tokens, micro - tokens, lower, SUB)

            @pl.when(jnp.logical_not(inner))
            def _():
                end_sends(step, lead)

            return carry

        lax.fori_loop(jnp.where(step < ahead, 1, 0), jnp.where(step < chunks, 2, 1), part, 0)
        refill(step)
        late = step - FIRST

        @pl.when(inner & (late >= 0) & (lax.rem(late + EVERY, EVERY) == 0))
        def _():
            turn_body(late // EVERY, 0)

        return carry

    for i in range(1, 4):
        input_copy(i).wait()

    to_normed(0, 0)
    opening()
    lax.fori_loop(1, steps, step_body, 0)

    if paired:
        @pl.when(jnp.logical_not(inner))
        def _():
            def held_send(chunk, carry):
                end_single(chunk)
                return carry

            lax.fori_loop(ahead, chunks, held_send, 0)

    @pl.when(inner)
    def _():
        done = jnp.maximum(steps - FIRST + EVERY - 1, 0) // EVERY
        lax.fori_loop(done, turns, turn_body, 0)

    natural = (place_of(mine) == 0) | (me == 1) | (me == last - 1)
    own_lines = lines_of(me, block)

    def final(index, carry):
        chunk = jnp.where(natural, index, lax.rem(index + ahead, chunks))

        @pl.when((me > 0) if not paired else (me > 0) & jnp.logical_not(leads))
        def _():
            single(chunk, me, True, me).wait_recv()

        @pl.when((me < last) if not paired else (me < last) & jnp.logical_not(trails))
        def _():
            single(chunk, me, False, me).wait_recv()

        columns = pl.ds(pl.multiple_of(chunk * width, width), width)
        preact = partial[chunk, own_lines].astype(jnp.float32) + bias_ref[:, columns]
        left = jnp.where(me > 0, received[chunk, landing(me + 1, block)].astype(jnp.float32), 0.0)
        right = jnp.where(me < last, received[chunk, landing(me, block)].astype(jnp.float32), 0.0)
        preact = preact + left + right
        out_ref[:, columns] = jax.nn.gelu(preact, approximate=True).astype(jnp.bfloat16)
        return carry

    def finish(i, carry):
        chunk, group = i // cols, lax.rem(i, cols)

        @pl.when(group != mine)
        def _():
            unit(chunk, group, True, me).wait_send()

        if paired:
            @pl.when(group == mine)
            def _():
                single(chunk, sibling, True, me).wait_send()

        return carry

    closing = min(CLOSING, chunks)
    lax.fori_loop(0, chunks - closing, final, 0)

    def finish_stat(i, carry):
        stat_copy(i).wait_send()
        return carry

    def finish_own(i, carry):
        own_copy(lax.rem(col + i, cols)).wait_send()
        return carry

    def finish_pass(i, carry):
        pass_copy(lax.rem(col + i, cols)).wait_send()
        return carry

    lax.fori_loop(0, rows * cols, finish_stat, 0)
    lax.fori_loop(0, direct, finish_own, 0)

    @pl.when(crossed)
    def _():
        lax.fori_loop(1, cols, finish_pass, 0)

    @pl.when(inner)
    def _():
        lax.fori_loop(0, chunks * cols, finish, 0)

    lax.fori_loop(chunks - closing, chunks, final, 0)

    @pl.when(jnp.logical_not(inner))
    def _():
        lax.fori_loop(0, chunks * cols, finish, 0)


def local(stages, rows, cols, handoff, norm_gain, norm_shift, up_weight, up_bias):
    own = handoff[0]
    tokens, depth = own.shape
    hidden = up_weight.shape[2]
    width = min(CHUNK, hidden)
    chunks = hidden // width
    micro = tokens * cols
    block = micro // rows
    result = pl.pallas_call(
        functools.partial(section_kernel, stages, rows, cols),
        out_shape=pltpu.VMEM((block, hidden), jnp.bfloat16),
        in_specs=[pl.BlockSpec(memory_space=pl.ANY)] * 5,
        out_specs=pl.BlockSpec(memory_space=pltpu.VMEM),
        scratch_shapes=[
            pltpu.VMEM((tokens, depth), jnp.bfloat16),
            pltpu.VMEM((1, depth), jnp.float32),
            pltpu.VMEM((1, depth), jnp.float32),
            pltpu.VMEM((1, hidden), jnp.float32),
            pltpu.VMEM((cols, tokens, depth), jnp.bfloat16),
            pltpu.VMEM((8, 128), jnp.float32),
            pltpu.VMEM((cols, rows, 8, 128), jnp.float32),
            pltpu.VMEM((micro, depth), jnp.bfloat16),
            pltpu.VMEM((SLOTS, depth, width), jnp.bfloat16),
            pltpu.VMEM((chunks, micro, width), jnp.bfloat16),
            pltpu.VMEM((chunks, (rows + 1) * block, width), jnp.bfloat16),
            pltpu.SemaphoreType.DMA((4,)),
            pltpu.SemaphoreType.DMA((SLOTS,)),
            pltpu.SemaphoreType.DMA((cols,)),
            pltpu.SemaphoreType.DMA((cols,)),
            pltpu.SemaphoreType.DMA((cols,)),
            pltpu.SemaphoreType.DMA((rows * cols,)),
            pltpu.SemaphoreType.DMA((cols, rows)),
            pltpu.SemaphoreType.DMA((chunks, rows)),
            pltpu.SemaphoreType.DMA((chunks, rows + 1)),
        ],
        compiler_params=pltpu.CompilerParams(
            collective_id=0, has_side_effects=True, vmem_limit_bytes=60 * 1024 * 1024
        ),
    )(own, norm_gain, norm_shift, up_weight[0], up_bias)
    return result[None]


def solution(mesh):
    in_specs = (
        P("pipe", "col", "row"),
        P("pipe", "row"),
        P("pipe", "row"),
        P("pipe", "row", "col"),
        P("pipe", "col"),
    )
    out_specs = P("pipe", "row", "col")
    sizes = mesh.shape["pipe"], mesh.shape["row"], mesh.shape["col"]
    return jax.shard_map(
        functools.partial(local, *sizes), mesh=mesh, in_specs=in_specs, out_specs=out_specs, check_vma=False
    )
```

```python
import functools

import jax
import jax.numpy as jnp
from jax import lax
from jax.experimental import pallas as pl
from jax.experimental.pallas import tpu as pltpu
from jax.sharding import PartitionSpec as P

epsilon = 1e-05
MESH = pl.DeviceIdType.MESH
CHUNK = 1024
SUB = 512
PARTS = 2
CLOSING = 3
SLOTS = 5
AHEAD = 6
AHEAD_CROSSED = 4
EVERY = 3
FIRST = 3


def section_kernel(
    stages, rows, cols,
    own_hbm, gain_hbm, shift_hbm, weight_ref, bias_hbm, out_ref,
    own_ref, gain_ref, shift_ref, bias_ref, landed, stats_out, stats_in, normed, weights, partial, received,
    input_sem, weight_sem, own_send, own_recv, pass_send, stat_send, stat_recv, part_send, part_recv,
):
    pipe, me, col = lax.axis_index("pipe"), lax.axis_index("row"), lax.axis_index("col")
    after = lax.rem(pipe + 1, stages)
    before = lax.rem(pipe + stages - 1, stages)
    tokens, depth = own_ref.shape
    chunks, parts, micro, span = partial.shape
    width = parts * span
    per_group = rows // cols
    block = tokens // per_group
    feature_count = depth * rows
    last = rows - 1
    crossed = lax.rem(pipe, 2) == 0
    ahead = jnp.where(crossed, min(AHEAD_CROSSED, chunks // 2), min(AHEAD, chunks // 2))
    lag = (ahead + 1) // 2
    steps = chunks + ahead
    turns = chunks + lag + max(rows - 3, 0)
    inner = (me > 0) & (me < last)
    mine = me // per_group
    paired = per_group == 2
    sibling = 2 * mine + 1 - lax.rem(me, 2)
    assert per_group <= 2
    direct = jnp.where(crossed, cols, 1)

    def weight_copy(step):
        chunk, slot = lax.rem(step, chunks), lax.rem(step, min(SLOTS, chunks))
        columns = pl.ds(pl.multiple_of(chunk * width, width), width)
        return pltpu.make_async_copy(weight_ref.at[:, columns], weights.at[slot], weight_sem.at[slot])

    def input_copy(i):
        source, target = ((own_hbm, own_ref), (gain_hbm, gain_ref), (shift_hbm, shift_ref), (bias_hbm, bias_ref))[i]
        return pltpu.make_async_copy(source, target, input_sem.at[i])

    for i in range(4):
        input_copy(i).start()

    barrier = pltpu.get_barrier_semaphore()

    def greet(i, carry):
        pl.semaphore_signal(
            barrier, inc=1, device_id=(before, i // cols, lax.rem(i, cols)), device_id_type=MESH
        )
        return carry

    lax.fori_loop(0, rows * cols, greet, 0)

    def greet_beside(i, carry):
        pl.semaphore_signal(barrier, inc=1, device_id=(pipe, me, lax.rem(col + i, cols)), device_id_type=MESH)
        return carry

    @pl.when(crossed)
    def _():
        lax.fori_loop(1, cols, greet_beside, 0)

    @pl.when(me > 0)
    def _():
        pl.semaphore_signal(barrier, inc=1, device_id=(pipe, me - 1, col), device_id_type=MESH)

    @pl.when(me < last)
    def _():
        pl.semaphore_signal(barrier, inc=1, device_id=(pipe, me + 1, col), device_id_type=MESH)

    for step in range(min(SLOTS, chunks)):
        weight_copy(step).start()

    input_copy(0).wait()
    total = jnp.zeros((tokens, 128), jnp.float32)
    squares = jnp.zeros((tokens, 128), jnp.float32)
    for lower in range(0, depth, 128):
        values = own_ref[:, lower:lower + 128].astype(jnp.float32)
        total = total + values
        squares = squares + values * values
    total = jnp.sum(total, axis=1, keepdims=True)
    squares = jnp.sum(squares, axis=1, keepdims=True)
    lane = lax.broadcasted_iota(jnp.int32, (tokens, 128), 1)
    both = jnp.where(lane == 0, total, jnp.where(lane == 1, squares, 0.0))
    if tokens < 128:
        both = jnp.concatenate([both, jnp.zeros((128 - tokens, 128), jnp.float32)], axis=0)
    stats_out[...] = both.T[:8]

    neighbours = (me > 0).astype(jnp.int32) + (me < last).astype(jnp.int32)
    pl.semaphore_wait(barrier, rows * cols + neighbours + jnp.where(crossed, cols - 1, 0))

    def own_copy(i):
        return pltpu.make_async_remote_copy(
            src_ref=own_ref, dst_ref=landed.at[col], send_sem=own_send.at[i], recv_sem=own_recv.at[col],
            device_id=(after, me, i), device_id_type=MESH,
        )

    def stat_copy(i):
        return pltpu.make_async_remote_copy(
            src_ref=stats_out, dst_ref=stats_in.at[col, me], send_sem=stat_send.at[i],
            recv_sem=stat_recv.at[col, me],
            device_id=(after, i // cols, lax.rem(i, cols)), device_id_type=MESH,
        )

    def start_stat(i, carry):
        stat_copy(i).start()
        return carry

    def start_own(i, carry):
        own_copy(lax.rem(col + i, cols)).start()
        return carry

    lax.fori_loop(0, rows * cols, start_stat, 0)
    lax.fori_loop(0, direct, start_own, 0)

    def pass_copy(i):
        return pltpu.make_async_remote_copy(
            src_ref=landed.at[col], dst_ref=landed.at[col], send_sem=pass_send.at[i], recv_sem=own_recv.at[col],
            device_id=(pipe, me, i), device_id_type=MESH,
        )

    def to_normed(place, carry):
        group = lax.rem(col + place, cols)

        def wait_stat(z, carry):
            pltpu.make_async_remote_copy(
                src_ref=stats_out, dst_ref=stats_in.at[group, z], send_sem=stat_send.at[0],
                recv_sem=stat_recv.at[group, z], device_id=(after, me, col), device_id_type=MESH,
            ).wait_recv()
            return carry + stats_in[group, z]

        sums = lax.fori_loop(0, rows, wait_stat, jnp.zeros((8, 128), jnp.float32))
        by_token = jnp.concatenate([sums, jnp.zeros((120, 128), jnp.float32)], axis=0).T[:tokens]
        center = by_token[:, 0:1] / feature_count
        inverse = lax.rsqrt(by_token[:, 1:2] / feature_count - center * center + epsilon)
        pltpu.make_async_remote_copy(
            src_ref=own_ref, dst_ref=landed.at[group], send_sem=own_send.at[0],
            recv_sem=own_recv.at[group], device_id=(after, me, col), device_id_type=MESH,
        ).wait_recv()

        @pl.when(crossed & (place == 0))
        def _():
            def start_pass(i, carry):
                pass_copy(lax.rem(col + i, cols)).start()
                return carry

            lax.fori_loop(1, cols, start_pass, 0)

        lines = pl.ds(pl.multiple_of(place * tokens, tokens), tokens)
        piece = 256
        for lower in range(0, depth, piece):
            part = landed[group, :, lower:lower + piece].astype(jnp.float32)
            scaled = (part - center) * inverse * gain_ref[:, lower:lower + piece]
            normed[lines, lower:lower + piece] = (scaled + shift_ref[:, lower:lower + piece]).astype(jnp.bfloat16)
        return carry

    def place_of(group):
        return lax.rem(group - col + cols, cols)

    def lines_of(first, count):
        start = place_of(first // per_group) * tokens + lax.rem(first, per_group) * block
        return pl.ds(pl.multiple_of(start, block), count)

    def landing(first, count):
        return pl.ds(pl.multiple_of(first * block, block), count)

    def piece_copy(chunk, first, count, up, target, which):
        place = first + jnp.where(up, 1, 0)
        return pltpu.make_async_remote_copy(
            src_ref=partial.at[chunk, which, lines_of(first, count)],
            dst_ref=received.at[chunk, which, landing(place, count)],
            send_sem=part_send.at[chunk, first], recv_sem=part_recv.at[chunk, place],
            device_id=(pipe, target, col), device_id_type=MESH,
        )

    everything = pl.ds(0, parts)

    def unit(chunk, group, up, target, which=everything):
        return piece_copy(chunk, group * per_group, tokens, up, target, which)

    def single(chunk, b, up, target, which=everything):
        return piece_copy(chunk, b, block, up, target, which)

    def chunk_of(group, index):
        return jnp.where(place_of(group) == 0, index, lax.rem(index + ahead, chunks))

    def add_arrived(chunk, first, count, up):
        lines = lines_of(first, count)
        spot = landing(first + jnp.where(up, 1, 0), count)
        for which in range(parts):
            own = partial[chunk, which, lines].astype(jnp.float32)
            arrived = received[chunk, which, spot].astype(jnp.float32)
            partial[chunk, which, lines] = (own + arrived).astype(jnp.bfloat16)

    leads, trails = lax.rem(me, per_group) == 0, lax.rem(me, per_group) == per_group - 1

    def relay_unit(chunk, group):
        up = group > mine
        unit(chunk, group, up, me).wait_recv()
        add_arrived(chunk, group * per_group, tokens, up)
        unit(chunk, group, up, jnp.where(up, me + 1, me - 1)).start()

    def relay_sibling(chunk):
        up = sibling > me
        unit(chunk, mine, up, me).wait_recv()
        add_arrived(chunk, sibling, block, up)
        single(chunk, sibling, up, sibling).start()

    def turn_body(turn, carry):
        def one(i, carry):
            group = jnp.where(lax.rem(i, 2) == 0, cols - 1 - i // 2, i // 2)
            up = jnp.where(group == mine, sibling > me, group > mine)
            hops = jnp.where(up, me - 1, last - 1 - me)
            index = turn - hops - jnp.where(place_of(group) == 0, 0, lag)
            valid = (index >= 0) & (index < chunks)

            @pl.when(valid & (group != mine))
            def _():
                relay_unit(chunk_of(group, index), group)

            if paired:
                @pl.when(valid & (group == mine))
                def _():
                    relay_sibling(chunk_of(group, index))

            return carry

        return lax.fori_loop(0, cols, one, carry)

    upward = me == 0
    beside = jnp.where(upward, 1, last - 1)

    def end_unit(chunk, group, which=everything):
        unit(chunk, group, upward, beside, which).start()

    def end_single(chunk, which=everything):
        single(chunk, sibling, upward, beside, which).start()

    def end_sends(step, lead):
        chunk = lax.rem(step, chunks)

        def one(i, carry):
            group = jnp.where(upward, cols - 1 - i, i)
            ready = (place_of(group) == 0) == lead

            @pl.when(ready & (group != mine))
            def _():
                end_unit(chunk, group)

            if paired:
                @pl.when(ready & (group == mine) & ((step < ahead) | (step >= chunks)))
                def _():
                    end_single(chunk)

            return carry

        lax.fori_loop(0, cols, one, 0)

    def multiply(chunk, slot, first, count, lower, extent):
        lines = pl.ds(first, count)
        product = jnp.dot(
            normed[lines, :], weights[slot, :, lower:lower + extent], preferred_element_type=jnp.float32
        )
        rounded = product.astype(jnp.bfloat16)
        for offset in range(0, extent, span):
            partial[chunk, (lower + offset) // span, lines] = rounded[:, offset:offset + span]

    def refill(step):
        @pl.when(step + min(SLOTS, chunks) < steps)
        def _():
            weight_copy(step + min(SLOTS, chunks)).start()

    def opening():
        weight_copy(0).wait()
        for index in range(parts):
            multiply(0, 0, 0, tokens, index * span, span)
            which = pl.ds(index, 1)

            @pl.when(jnp.logical_not(inner) & (mine != col))
            def _():
                end_unit(0, col, which)

            if paired:
                @pl.when(jnp.logical_not(inner) & (mine == col))
                def _():
                    end_single(0, which)

        refill(0)

    def step_body(step, carry):
        chunk, slot = lax.rem(step, chunks), lax.rem(step, min(SLOTS, chunks))

        @pl.when(step == ahead)
        def _():
            lax.fori_loop(1, cols, to_normed, 0)

        weight_copy(step).wait()

        def part(which, carry):
            lead = which == 1
            if micro == 2 * tokens:
                first = pl.multiple_of(jnp.where(lead, 0, tokens), tokens)
                for lower in range(0, width, SUB):
                    multiply(chunk, slot, first, tokens, lower, SUB)
            else:
                @pl.when(lead)
                def _():
                    for lower in range(0, width, SUB):
                        multiply(chunk, slot, 0, tokens, lower, SUB)

                @pl.when(jnp.logical_not(lead))
                def _():
                    for lower in range(0, width, SUB):
                        multiply(chunk, slot, tokens, micro - tokens, lower, SUB)

            @pl.when(jnp.logical_not(inner))
            def _():
                end_sends(step, lead)

            return carry

        lax.fori_loop(jnp.where(step < ahead, 1, 0), jnp.where(step < chunks, 2, 1), part, 0)
        refill(step)
        late = step - FIRST

        @pl.when(inner & (late >= 0) & (lax.rem(late + EVERY, EVERY) == 0))
        def _():
            turn_body(late // EVERY, 0)

        return carry

    for i in range(1, 4):
        input_copy(i).wait()

    to_normed(0, 0)
    opening()
    lax.fori_loop(1, steps, step_body, 0)

    if paired:
        @pl.when(jnp.logical_not(inner))
        def _():
            def held_send(chunk, carry):
                end_single(chunk)
                return carry

            lax.fori_loop(ahead, chunks, held_send, 0)

    @pl.when(inner)
    def _():
        done = jnp.maximum(steps - FIRST + EVERY - 1, 0) // EVERY
        lax.fori_loop(done, turns, turn_body, 0)

    natural = (place_of(mine) == 0) | (me == 1) | (me == last - 1)
    own_lines = lines_of(me, block)

    def final(index, carry):
        chunk = jnp.where(natural, index, lax.rem(index + ahead, chunks))

        @pl.when((me > 0) if not paired else (me > 0) & jnp.logical_not(leads))
        def _():
            single(chunk, me, True, me).wait_recv()

        @pl.when((me < last) if not paired else (me < last) & jnp.logical_not(trails))
        def _():
            single(chunk, me, False, me).wait_recv()

        for which in range(parts):
            columns = pl.ds(pl.multiple_of(chunk * width + which * span, span), span)
            preact = partial[chunk, which, own_lines].astype(jnp.float32) + bias_ref[:, columns]
            left = jnp.where(me > 0, received[chunk, which, landing(me + 1, block)].astype(jnp.float32), 0.0)
            right = jnp.where(me < last, received[chunk, which, landing(me, block)].astype(jnp.float32), 0.0)
            preact = preact + left + right
            out_ref[:, columns] = jax.nn.gelu(preact, approximate=True).astype(jnp.bfloat16)
        return carry

    def finish(i, carry):
        chunk, group = i // cols, lax.rem(i, cols)

        @pl.when(group != mine)
        def _():
            unit(chunk, group, True, me).wait_send()

        if paired:
            @pl.when(group == mine)
            def _():
                single(chunk, sibling, True, me).wait_send()

        return carry

    closing = min(CLOSING, chunks)
    lax.fori_loop(0, chunks - closing, final, 0)

    def finish_stat(i, carry):
        stat_copy(i).wait_send()
        return carry

    def finish_own(i, carry):
        own_copy(lax.rem(col + i, cols)).wait_send()
        return carry

    def finish_pass(i, carry):
        pass_copy(lax.rem(col + i, cols)).wait_send()
        return carry

    lax.fori_loop(0, rows * cols, finish_stat, 0)
    lax.fori_loop(0, direct, finish_own, 0)

    @pl.when(crossed)
    def _():
        lax.fori_loop(1, cols, finish_pass, 0)

    @pl.when(inner)
    def _():
        lax.fori_loop(0, chunks * cols, finish, 0)

    lax.fori_loop(chunks - closing, chunks, final, 0)

    @pl.when(jnp.logical_not(inner))
    def _():
        lax.fori_loop(0, chunks * cols, finish, 0)


def local(stages, rows, cols, handoff, norm_gain, norm_shift, up_weight, up_bias):
    own = handoff[0]
    tokens, depth = own.shape
    hidden = up_weight.shape[2]
    width = min(CHUNK, hidden)
    chunks = hidden // width
    micro = tokens * cols
    block = micro // rows
    result = pl.pallas_call(
        functools.partial(section_kernel, stages, rows, cols),
        out_shape=pltpu.VMEM((block, hidden), jnp.bfloat16),
        in_specs=[pl.BlockSpec(memory_space=pl.ANY)] * 5,
        out_specs=pl.BlockSpec(memory_space=pltpu.VMEM),
        scratch_shapes=[
            pltpu.VMEM((tokens, depth), jnp.bfloat16),
            pltpu.VMEM((1, depth), jnp.float32),
            pltpu.VMEM((1, depth), jnp.float32),
            pltpu.VMEM((1, hidden), jnp.float32),
            pltpu.VMEM((cols, tokens, depth), jnp.bfloat16),
            pltpu.VMEM((8, 128), jnp.float32),
            pltpu.VMEM((cols, rows, 8, 128), jnp.float32),
            pltpu.VMEM((micro, depth), jnp.bfloat16),
            pltpu.VMEM((SLOTS, depth, width), jnp.bfloat16),
            pltpu.VMEM((chunks, PARTS, micro, width // PARTS), jnp.bfloat16),
            pltpu.VMEM((chunks, PARTS, (rows + 1) * block, width // PARTS), jnp.bfloat16),
            pltpu.SemaphoreType.DMA((4,)),
            pltpu.SemaphoreType.DMA((SLOTS,)),
            pltpu.SemaphoreType.DMA((cols,)),
            pltpu.SemaphoreType.DMA((cols,)),
            pltpu.SemaphoreType.DMA((cols,)),
            pltpu.SemaphoreType.DMA((rows * cols,)),
            pltpu.SemaphoreType.DMA((cols, rows)),
            pltpu.SemaphoreType.DMA((chunks, rows)),
            pltpu.SemaphoreType.DMA((chunks, rows + 1)),
        ],
        compiler_params=pltpu.CompilerParams(
            collective_id=0, has_side_effects=True, vmem_limit_bytes=60 * 1024 * 1024
        ),
    )(own, norm_gain, norm_shift, up_weight[0], up_bias)
    return result[None]


def solution(mesh):
    in_specs = (
        P("pipe", "col", "row"),
        P("pipe", "row"),
        P("pipe", "row"),
        P("pipe", "row", "col"),
        P("pipe", "col"),
    )
    out_specs = P("pipe", "row", "col")
    sizes = mesh.shape["pipe"], mesh.shape["row"], mesh.shape["col"]
    return jax.shard_map(
        functools.partial(local, *sizes), mesh=mesh, in_specs=in_specs, out_specs=out_specs, check_vma=False
    )
```

```python
import functools

import jax
import jax.numpy as jnp
from jax import lax
from jax.experimental import pallas as pl
from jax.experimental.pallas import tpu as pltpu
from jax.sharding import PartitionSpec as P

epsilon = 1e-05
MESH = pl.DeviceIdType.MESH
CHUNK = 1024
SUB = 512
PARTS = 2
CLOSING = 6
SLOTS = 5
AHEAD = 6
AHEAD_CROSSED = 4
EVERY = 2
FIRST = 3


def section_kernel(
    stages, rows, cols,
    own_hbm, gain_hbm, shift_hbm, weight_ref, bias_hbm, out_ref,
    own_ref, gain_ref, shift_ref, bias_ref, landed, stats_out, stats_in, normed, weights, partial, received,
    input_sem, weight_sem, own_send, own_recv, pass_send, stat_send, stat_recv, part_send, part_recv,
):
    pipe, me, col = lax.axis_index("pipe"), lax.axis_index("row"), lax.axis_index("col")
    after = lax.rem(pipe + 1, stages)
    before = lax.rem(pipe + stages - 1, stages)
    tokens, depth = own_ref.shape
    chunks, parts, micro, span = partial.shape
    width = parts * span
    per_group = rows // cols
    block = tokens // per_group
    feature_count = depth * rows
    last = rows - 1
    crossed = lax.rem(pipe, 2) == 0
    ahead = jnp.where(crossed, min(AHEAD_CROSSED, chunks // 2), min(AHEAD, chunks // 2))
    lag = (ahead + 1) // 2
    steps = chunks + ahead
    turns = chunks + lag + max(rows - 3, 0)
    inner = (me > 0) & (me < last)
    mine = me // per_group
    paired = per_group == 2
    sibling = 2 * mine + 1 - lax.rem(me, 2)
    assert per_group <= 2
    direct = jnp.where(crossed, cols, 1)

    def weight_copy(step):
        chunk, slot = lax.rem(step, chunks), lax.rem(step, min(SLOTS, chunks))
        columns = pl.ds(pl.multiple_of(chunk * width, width), width)
        return pltpu.make_async_copy(weight_ref.at[:, columns], weights.at[slot], weight_sem.at[slot])

    def input_copy(i):
        source, target = ((own_hbm, own_ref), (gain_hbm, gain_ref), (shift_hbm, shift_ref), (bias_hbm, bias_ref))[i]
        return pltpu.make_async_copy(source, target, input_sem.at[i])

    for i in range(4):
        input_copy(i).start()

    barrier = pltpu.get_barrier_semaphore()

    def greet(i, carry):
        pl.semaphore_signal(
            barrier, inc=1, device_id=(before, i // cols, lax.rem(i, cols)), device_id_type=MESH
        )
        return carry

    lax.fori_loop(0, rows * cols, greet, 0)

    def greet_beside(i, carry):
        pl.semaphore_signal(barrier, inc=1, device_id=(pipe, me, lax.rem(col + i, cols)), device_id_type=MESH)
        return carry

    @pl.when(crossed)
    def _():
        lax.fori_loop(1, cols, greet_beside, 0)

    @pl.when(me > 0)
    def _():
        pl.semaphore_signal(barrier, inc=1, device_id=(pipe, me - 1, col), device_id_type=MESH)

    @pl.when(me < last)
    def _():
        pl.semaphore_signal(barrier, inc=1, device_id=(pipe, me + 1, col), device_id_type=MESH)

    for step in range(min(SLOTS, chunks)):
        weight_copy(step).start()

    input_copy(0).wait()
    total = jnp.zeros((tokens, 128), jnp.float32)
    squares = jnp.zeros((tokens, 128), jnp.float32)
    for lower in range(0, depth, 128):
        values = own_ref[:, lower:lower + 128].astype(jnp.float32)
        total = total + values
        squares = squares + values * values
    total = jnp.sum(total, axis=1, keepdims=True)
    squares = jnp.sum(squares, axis=1, keepdims=True)
    lane = lax.broadcasted_iota(jnp.int32, (tokens, 128), 1)
    both = jnp.where(lane == 0, total, jnp.where(lane == 1, squares, 0.0))
    if tokens < 128:
        both = jnp.concatenate([both, jnp.zeros((128 - tokens, 128), jnp.float32)], axis=0)
    stats_out[...] = both.T[:8]

    neighbours = (me > 0).astype(jnp.int32) + (me < last).astype(jnp.int32)
    pl.semaphore_wait(barrier, rows * cols + neighbours + jnp.where(crossed, cols - 1, 0))

    def own_copy(i):
        return pltpu.make_async_remote_copy(
            src_ref=own_ref, dst_ref=landed.at[col], send_sem=own_send.at[i], recv_sem=own_recv.at[col],
            device_id=(after, me, i), device_id_type=MESH,
        )

    def stat_copy(i):
        return pltpu.make_async_remote_copy(
            src_ref=stats_out, dst_ref=stats_in.at[col, me], send_sem=stat_send.at[i],
            recv_sem=stat_recv.at[col, me],
            device_id=(after, i // cols, lax.rem(i, cols)), device_id_type=MESH,
        )

    def start_stat(i, carry):
        stat_copy(i).start()
        return carry

    def start_own(i, carry):
        own_copy(lax.rem(col + i, cols)).start()
        return carry

    lax.fori_loop(0, rows * cols, start_stat, 0)
    lax.fori_loop(0, direct, start_own, 0)

    def pass_copy(i):
        return pltpu.make_async_remote_copy(
            src_ref=landed.at[col], dst_ref=landed.at[col], send_sem=pass_send.at[i], recv_sem=own_recv.at[col],
            device_id=(pipe, me, i), device_id_type=MESH,
        )

    def to_normed(place, carry):
        group = lax.rem(col + place, cols)

        def wait_stat(z, carry):
            pltpu.make_async_remote_copy(
                src_ref=stats_out, dst_ref=stats_in.at[group, z], send_sem=stat_send.at[0],
                recv_sem=stat_recv.at[group, z], device_id=(after, me, col), device_id_type=MESH,
            ).wait_recv()
            return carry + stats_in[group, z]

        sums = lax.fori_loop(0, rows, wait_stat, jnp.zeros((8, 128), jnp.float32))
        by_token = jnp.concatenate([sums, jnp.zeros((120, 128), jnp.float32)], axis=0).T[:tokens]
        center = by_token[:, 0:1] / feature_count
        inverse = lax.rsqrt(by_token[:, 1:2] / feature_count - center * center + epsilon)
        pltpu.make_async_remote_copy(
            src_ref=own_ref, dst_ref=landed.at[group], send_sem=own_send.at[0],
            recv_sem=own_recv.at[group], device_id=(after, me, col), device_id_type=MESH,
        ).wait_recv()

        @pl.when(crossed & (place == 0))
        def _():
            def start_pass(i, carry):
                pass_copy(lax.rem(col + i, cols)).start()
                return carry

            lax.fori_loop(1, cols, start_pass, 0)

        lines = pl.ds(pl.multiple_of(place * tokens, tokens), tokens)
        piece = 256
        for lower in range(0, depth, piece):
            part = landed[group, :, lower:lower + piece].astype(jnp.float32)
            scaled = (part - center) * inverse * gain_ref[:, lower:lower + piece]
            normed[lines, lower:lower + piece] = (scaled + shift_ref[:, lower:lower + piece]).astype(jnp.bfloat16)
        return carry

    def place_of(group):
        return lax.rem(group - col + cols, cols)

    def lines_of(first, count):
        start = place_of(first // per_group) * tokens + lax.rem(first, per_group) * block
        return pl.ds(pl.multiple_of(start, block), count)

    def landing(first, count):
        return pl.ds(pl.multiple_of(first * block, block), count)

    def piece_copy(chunk, first, count, up, target, which):
        place = first + jnp.where(up, 1, 0)
        return pltpu.make_async_remote_copy(
            src_ref=partial.at[chunk, which, lines_of(first, count)],
            dst_ref=received.at[chunk, which, landing(place, count)],
            send_sem=part_send.at[chunk, first], recv_sem=part_recv.at[chunk, place],
            device_id=(pipe, target, col), device_id_type=MESH,
        )

    everything = pl.ds(0, parts)

    def unit(chunk, group, up, target, which=everything):
        return piece_copy(chunk, group * per_group, tokens, up, target, which)

    def single(chunk, b, up, target, which=everything):
        return piece_copy(chunk, b, block, up, target, which)

    def chunk_of(group, index):
        return jnp.where(place_of(group) == 0, index, lax.rem(index + ahead, chunks))

    def add_arrived(chunk, first, count, up):
        lines = lines_of(first, count)
        spot = landing(first + jnp.where(up, 1, 0), count)
        for which in range(parts):
            own = partial[chunk, which, lines].astype(jnp.float32)
            arrived = received[chunk, which, spot].astype(jnp.float32)
            partial[chunk, which, lines] = (own + arrived).astype(jnp.bfloat16)

    leads, trails = lax.rem(me, per_group) == 0, lax.rem(me, per_group) == per_group - 1

    def relay_unit(chunk, group):
        up = group > mine
        unit(chunk, group, up, me).wait_recv()
        add_arrived(chunk, group * per_group, tokens, up)
        unit(chunk, group, up, jnp.where(up, me + 1, me - 1)).start()

    def relay_sibling(chunk):
        up = sibling > me
        unit(chunk, mine, up, me).wait_recv()
        add_arrived(chunk, sibling, block, up)
        single(chunk, sibling, up, sibling).start()

    def turn_body(turn, carry):
        def one(i, carry):
            group = jnp.where(lax.rem(i, 2) == 0, cols - 1 - i // 2, i // 2)
            up = jnp.where(group == mine, sibling > me, group > mine)
            hops = jnp.where(up, me - 1, last - 1 - me)
            index = turn - hops - jnp.where(place_of(group) == 0, 0, lag)
            valid = (index >= 0) & (index < chunks)

            @pl.when(valid & (group != mine))
            def _():
                relay_unit(chunk_of(group, index), group)

            if paired:
                @pl.when(valid & (group == mine))
                def _():
                    relay_sibling(chunk_of(group, index))

            return carry

        return lax.fori_loop(0, cols, one, carry)

    upward = me == 0
    beside = jnp.where(upward, 1, last - 1)

    def end_unit(chunk, group, which=everything):
        unit(chunk, group, upward, beside, which).start()

    def end_single(chunk, which=everything):
        single(chunk, sibling, upward, beside, which).start()

    def end_sends(step, lead):
        chunk = lax.rem(step, chunks)

        def one(i, carry):
            group = jnp.where(upward, cols - 1 - i, i)
            ready = (place_of(group) == 0) == lead

            @pl.when(ready & (group != mine))
            def _():
                end_unit(chunk, group)

            if paired:
                @pl.when(ready & (group == mine) & ((step < ahead) | (step >= chunks)))
                def _():
                    end_single(chunk)

            return carry

        lax.fori_loop(0, cols, one, 0)

    def multiply(chunk, slot, first, count, lower, extent):
        lines = pl.ds(first, count)
        product = jnp.dot(
            normed[lines, :], weights[slot, :, lower:lower + extent], preferred_element_type=jnp.float32
        )
        rounded = product.astype(jnp.bfloat16)
        for offset in range(0, extent, span):
            partial[chunk, (lower + offset) // span, lines] = rounded[:, offset:offset + span]

    def refill(step):
        @pl.when(step + min(SLOTS, chunks) < steps)
        def _():
            weight_copy(step + min(SLOTS, chunks)).start()

    def opening():
        weight_copy(0).wait()
        for index in range(parts):
            multiply(0, 0, 0, tokens, index * span, span)
            which = pl.ds(index, 1)

            @pl.when(jnp.logical_not(inner) & (mine != col))
            def _():
                end_unit(0, col, which)

            if paired:
                @pl.when(jnp.logical_not(inner) & (mine == col))
                def _():
                    end_single(0, which)

        refill(0)

    def step_body(step, carry):
        chunk, slot = lax.rem(step, chunks), lax.rem(step, min(SLOTS, chunks))

        @pl.when(step == ahead)
        def _():
            lax.fori_loop(1, cols, to_normed, 0)

        weight_copy(step).wait()

        def part(which, carry):
            lead = which == 1
            if micro == 2 * tokens:
                first = pl.multiple_of(jnp.where(lead, 0, tokens), tokens)
                for lower in range(0, width, SUB):
                    multiply(chunk, slot, first, tokens, lower, SUB)
            else:
                @pl.when(lead)
                def _():
                    for lower in range(0, width, SUB):
                        multiply(chunk, slot, 0, tokens, lower, SUB)

                @pl.when(jnp.logical_not(lead))
                def _():
                    for lower in range(0, width, SUB):
                        multiply(chunk, slot, tokens, micro - tokens, lower, SUB)

            @pl.when(jnp.logical_not(inner))
            def _():
                end_sends(step, lead)

            return carry

        lax.fori_loop(jnp.where(step < ahead, 1, 0), jnp.where(step < chunks, 2, 1), part, 0)
        refill(step)
        late = step - FIRST

        @pl.when(inner & (late >= 0) & (lax.rem(late + EVERY, EVERY) == 0))
        def _():
            turn_body(late // EVERY, 0)

        return carry

    for i in range(1, 4):
        input_copy(i).wait()

    to_normed(0, 0)
    opening()
    lax.fori_loop(1, steps, step_body, 0)

    if paired:
        @pl.when(jnp.logical_not(inner))
        def _():
            def held_send(chunk, carry):
                end_single(chunk)
                return carry

            lax.fori_loop(ahead, chunks, held_send, 0)

    @pl.when(inner)
    def _():
        done = jnp.maximum(steps - FIRST + EVERY - 1, 0) // EVERY
        lax.fori_loop(done, turns, turn_body, 0)

    natural = (place_of(mine) == 0) | (me == 1) | (me == last - 1)
    own_lines = lines_of(me, block)

    def final(index, carry):
        chunk = jnp.where(natural, index, lax.rem(index + ahead, chunks))

        @pl.when((me > 0) if not paired else (me > 0) & jnp.logical_not(leads))
        def _():
            single(chunk, me, True, me).wait_recv()

        @pl.when((me < last) if not paired else (me < last) & jnp.logical_not(trails))
        def _():
            single(chunk, me, False, me).wait_recv()

        for which in range(parts):
            columns = pl.ds(pl.multiple_of(chunk * width + which * span, span), span)
            preact = partial[chunk, which, own_lines].astype(jnp.float32) + bias_ref[:, columns]
            left = jnp.where(me > 0, received[chunk, which, landing(me + 1, block)].astype(jnp.float32), 0.0)
            right = jnp.where(me < last, received[chunk, which, landing(me, block)].astype(jnp.float32), 0.0)
            preact = preact + left + right
            out_ref[:, columns] = jax.nn.gelu(preact, approximate=True).astype(jnp.bfloat16)
        return carry

    def finish(i, carry):
        chunk, group = i // cols, lax.rem(i, cols)

        @pl.when(group != mine)
        def _():
            unit(chunk, group, True, me).wait_send()

        if paired:
            @pl.when(group == mine)
            def _():
                single(chunk, sibling, True, me).wait_send()

        return carry

    closing = min(CLOSING, chunks)
    lax.fori_loop(0, chunks - closing, final, 0)

    def finish_stat(i, carry):
        stat_copy(i).wait_send()
        return carry

    def finish_own(i, carry):
        own_copy(lax.rem(col + i, cols)).wait_send()
        return carry

    def finish_pass(i, carry):
        pass_copy(lax.rem(col + i, cols)).wait_send()
        return carry

    lax.fori_loop(0, rows * cols, finish_stat, 0)
    lax.fori_loop(0, direct, finish_own, 0)

    @pl.when(crossed)
    def _():
        lax.fori_loop(1, cols, finish_pass, 0)

    @pl.when(inner)
    def _():
        lax.fori_loop(0, chunks * cols, finish, 0)

    lax.fori_loop(chunks - closing, chunks, final, 0)

    @pl.when(jnp.logical_not(inner))
    def _():
        lax.fori_loop(0, chunks * cols, finish, 0)


def local(stages, rows, cols, handoff, norm_gain, norm_shift, up_weight, up_bias):
    own = handoff[0]
    tokens, depth = own.shape
    hidden = up_weight.shape[2]
    width = min(CHUNK, hidden)
    chunks = hidden // width
    micro = tokens * cols
    block = micro // rows
    result = pl.pallas_call(
        functools.partial(section_kernel, stages, rows, cols),
        out_shape=pltpu.VMEM((block, hidden), jnp.bfloat16),
        in_specs=[pl.BlockSpec(memory_space=pl.ANY)] * 5,
        out_specs=pl.BlockSpec(memory_space=pltpu.VMEM),
        scratch_shapes=[
            pltpu.VMEM((tokens, depth), jnp.bfloat16),
            pltpu.VMEM((1, depth), jnp.float32),
            pltpu.VMEM((1, depth), jnp.float32),
            pltpu.VMEM((1, hidden), jnp.float32),
            pltpu.VMEM((cols, tokens, depth), jnp.bfloat16),
            pltpu.VMEM((8, 128), jnp.float32),
            pltpu.VMEM((cols, rows, 8, 128), jnp.float32),
            pltpu.VMEM((micro, depth), jnp.bfloat16),
            pltpu.VMEM((SLOTS, depth, width), jnp.bfloat16),
            pltpu.VMEM((chunks, PARTS, micro, width // PARTS), jnp.bfloat16),
            pltpu.VMEM((chunks, PARTS, (rows + 1) * block, width // PARTS), jnp.bfloat16),
            pltpu.SemaphoreType.DMA((4,)),
            pltpu.SemaphoreType.DMA((SLOTS,)),
            pltpu.SemaphoreType.DMA((cols,)),
            pltpu.SemaphoreType.DMA((cols,)),
            pltpu.SemaphoreType.DMA((cols,)),
            pltpu.SemaphoreType.DMA((rows * cols,)),
            pltpu.SemaphoreType.DMA((cols, rows)),
            pltpu.SemaphoreType.DMA((chunks, rows)),
            pltpu.SemaphoreType.DMA((chunks, rows + 1)),
        ],
        compiler_params=pltpu.CompilerParams(
            collective_id=0, has_side_effects=True, vmem_limit_bytes=60 * 1024 * 1024
        ),
    )(own, norm_gain, norm_shift, up_weight[0], up_bias)
    return result[None]


def solution(mesh):
    in_specs = (
        P("pipe", "col", "row"),
        P("pipe", "row"),
        P("pipe", "row"),
        P("pipe", "row", "col"),
        P("pipe", "col"),
    )
    out_specs = P("pipe", "row", "col")
    sizes = mesh.shape["pipe"], mesh.shape["row"], mesh.shape["col"]
    return jax.shard_map(
        functools.partial(local, *sizes), mesh=mesh, in_specs=in_specs, out_specs=out_specs, check_vma=False
    )
```
